128 devices in a mesh: tm: 16 (over z, x_hi, core), space: 8 (over x_lo, y).
Axes of the slice: x: 4 (x_hi: 2, x_lo: 2; x = x_hi * 2 + x_lo), y: 4, z: 4, core: 2. Of those that a mesh axis runs over, the one named last changes fastest.
Arguments:
- initial: float32 [128, 128, 2048], P('tm', 'space'), may hold values from -6 to 6
- source: float32 [128, 128, 2048], P('tm', 'space'), may hold values from -3 to 3.3
- diffusivity: float32 [128, 2048], P('space'), may hold values from 0.3 to 1
- growth: float32 [128, 2048], P('space'), may hold values from 0.5 to 4
Outputs:
- solution: float32 [128, 128, 2048], P('tm', 'space')
The draws below stay inside these ranges and needn't reach their ends.
All inputs are finite; a program needn't handle non-finite values.
Results may differ from the reference program's by a relative error of at most 0.00002.
Values sent between devices are 32-bit elements; how exact they have to be, the bound alone decides.
A program may use at most 64 MiB of HBM per device.

```python
import math
import jax
import jax.numpy as jnp
from jax import lax

COLS = 2048
LEVELS = 4
STEPS_ALL = 128
GRID_ROWS = 128


def draw_source(key, part):
    second_key = jax.random.fold_in(key, 1)
    shape = (STEPS_ALL, GRID_ROWS, COLS)
    rough = 0.5 * jax.random.normal(second_key, shape, jnp.float32)
    return jnp.clip(rough, -3.0, 3.3)


def level_of(stream_key, shape, shards, low, high):
    def one(position, shards_of):
        steps = jax.random.uniform(jax.random.fold_in(jax.random.fold_in(stream_key, 6), position), (shards_of,), jnp.float32, low / len(shards), high / len(shards))
        return jnp.repeat(jnp.exp(steps), shape[position] // shards_of).reshape((-1,) + (1,) * (len(shape) - position - 1))

    level = one(*shards[0])
    for cut in shards[1:]:
        level = level * one(*cut)
    return level


def centred(rng, extent, deviation, bound, cuts=(), kind=jnp.bfloat16):
    values = jax.random.normal(rng, extent, jnp.float32) * deviation
    if len(cuts) > 0:
        values = level_of(rng, extent, cuts, -0.22, 0.18) * values
    return jnp.clip(values, min=-bound, max=bound).astype(kind)


def setup_inputs(seed: int = 0) -> dict:
    streams_of = jax.random.split(jax.random.key(seed), 5)
    return {
        "initial": centred(streams_of[0], (STEPS_ALL, GRID_ROWS, COLS), 1.0, 6.0, ((0, 16), (1, 8)), jnp.float32),
        "source": draw_source(jax.random.fold_in(streams_of[4], 71), 0),
        "diffusivity": jnp.clip(jnp.exp(math.log(1.0) - 1.2039728 * jax.random.uniform(streams_of[2], (GRID_ROWS, COLS), jnp.float32) ** level_of(streams_of[2], (GRID_ROWS, COLS), ((0, 8),), -0.2, 0.2)), 0.3, 1.0),
        "growth": jnp.clip(jnp.exp(math.log(4.0) - 2.0794415 * jax.random.uniform(streams_of[3], (GRID_ROWS, COLS), jnp.float32) ** level_of(streams_of[3], (GRID_ROWS, COLS), ((0, 8),), -0.2, 0.2)), 0.5, 4.0),
    }


diffusion_number = 0.03
time_step = 0.02


def propagate(fields, scales, diffusivity, growth):
    padded = jnp.pad(fields, ((0, 0), (1, 1), (1, 1)))
    beside_all = padded[:, :-2, 1:-1] + padded[:, 2:, 1:-1] + padded[:, 1:-1, :-2] + padded[:, 1:-1, 2:]
    laplace = beside_all - 4.0 * fields
    factor = scales[:, None, None]
    return fields + (diffusion_number * factor) * diffusivity * laplace + (time_step * factor) * growth * fields / (1.0 + fields * fields)


def uniform_scales(count, level_index):
    return jnp.full((count,), 2.0 ** level_index, jnp.float32)


def coarsest(states, forcing, diffusivity, growth):
    unit = uniform_scales(1, LEVELS - 1)

    def advance(prior, term):
        following = propagate(prior, unit, diffusivity, growth) + term[None]
        return following, following[0]

    final_state, chain = lax.scan(advance, states[-1:], forcing)
    return chain


def cycle(level_index, states, forcing, diffusivity, growth):
    if level_index == LEVELS - 1:
        return coarsest(states, forcing, diffusivity, growth)
    half = states.shape[0] // 2
    scales = uniform_scales(half, level_index)
    even_forcing = forcing[0::2]
    odd_forcing = forcing[1::2]
    even_points = states[0::2]
    odd_points = propagate(even_points, scales, diffusivity, growth) + odd_forcing
    shifted = jnp.concatenate([odd_points[-1:], odd_points[:-1]], axis=0)
    even_points = propagate(shifted, scales, diffusivity, growth) + even_forcing
    odd_points = propagate(even_points, scales, diffusivity, growth) + odd_forcing
    both_scales = jnp.concatenate([scales, uniform_scales(half, level_index + 1)])
    images = propagate(jnp.concatenate([odd_points, even_points], axis=0), both_scales, diffusivity, growth)
    pair_terms = images[:half] - images[half:]
    reduced_forcing = even_forcing + jnp.concatenate([pair_terms[-1:], pair_terms[:-1]], axis=0)
    coarse_points = cycle(level_index + 1, even_points, reduced_forcing, diffusivity, growth)
    odd_points = propagate(coarse_points, scales, diffusivity, growth) + odd_forcing
    return jnp.stack([coarse_points, odd_points], axis=1).reshape(states.shape)


def reference(initial, source, diffusivity, growth):
    return cycle(0, initial, source, diffusivity, growth)
```

```python
import functools

import jax
import jax.numpy as jnp
from jax import lax
from jax.experimental import pallas as pl
from jax.experimental.pallas import tpu as pltpu
from jax.sharding import PartitionSpec as P

MESH = pl.DeviceIdType.MESH
F32 = jnp.float32
DIFFUSION = 0.03
STEP = 0.02

OWN = 16
BUF = 24
LANES = 128
GROUP = 4
PAIRS = (4, 2, 1)

_names = [
    ("v0", 3), ("dif", 3), ("gro", 3), ("ge0", 3), ("go0", 3),
    ("o1_0", 3), ("o1_1", 3), ("ge1", 3), ("go1", 3), ("go2", 3),
    ("po0", 3), ("po1", 3), ("po2", 3), ("pr0", 3), ("pr1", 3),
    ("ga", 12), ("gb", 12), ("vin", 3), ("vr", 12), ("old", 12),
]
SEM = {}
_at = 0
for _name, _count in _names:
    SEM[_name] = _at
    _at += _count
N_SEM = _at


def kernel(n_t, n_s, cols, ini, src, dif, gro, out, v0, ge0, ge1, ge2, go0, go1, go2, o10, o11, o12,
           po, pr, ee, ne, ob, ps, dd, rr, aa, bb, xa, xb, xv, ga, gb, vin, vo, ap, bp, vr, res,
           ss, rs, ls):
    ge, go, o1 = (ge0, ge1, ge2), (go0, go1, go2), (o10, o11, o12)
    width = cols // GROUP
    wide = width + LANES
    t, s = lax.axis_index("tm"), lax.axis_index("space")
    z, q = t // GROUP, lax.rem(t, GROUP)
    nz = n_t // GROUP
    following = lax.rem(t + 1, n_t)
    has_up, has_down = s > 0, s < n_s - 1
    sent = []

    def when(cond, fn):
        if cond is None:
            fn()
        else:
            pl.when(cond)(fn)

    def both(a, b):
        return b if a is None else (a if b is None else jnp.logical_and(a, b))

    def send(source, target, si, ri, tm, space, cond=None):
        def copy():
            return pltpu.make_async_remote_copy(
                src_ref=source, dst_ref=target, send_sem=ss.at[si], recv_sem=rs.at[ri],
                device_id={"tm": tm, "space": space}, device_id_type=MESH)
        when(cond, lambda: copy().start())
        sent.append((cond, copy))

    def send_edges(source, target, h, si, ri, tm, cond=None):
        send(source(OWN - h, h), target(BUF - h, h), si + 1, ri + 1, tm, s + 1, both(cond, has_down))
        send(source(0, h), target(OWN, h), si + 2, ri + 2, tm, s - 1, both(cond, has_up))

    def arrived(target, ri, cond=None):
        def wait():
            pltpu.make_async_remote_copy(
                src_ref=target, dst_ref=target, send_sem=ss.at[0], recv_sem=rs.at[ri],
                device_id={"tm": following, "space": s}, device_id_type=MESH).wait_recv()
        when(cond, wait)

    def edges_arrived(target, h, ri):
        arrived(target(BUF - h, h), ri + 1, has_up)
        arrived(target(OWN, h), ri + 2, has_down)

    def all_arrived(target, h, ri):
        arrived(target(0, OWN), ri)
        edges_arrived(target, h, ri)

    def rows_of(ref, *lead):
        return lambda r, h: ref.at[(*lead, pl.ds(r, h), slice(None))]

    loads = []

    def load(source, target):
        copy = pltpu.make_async_copy(source, target, ls.at[len(loads)])
        copy.start()
        loads.append(copy)

    for j in range(4):
        load(ini.at[2 * j], v0.at[j, 0:OWN, :])
    load(dif, dd.at[0:OWN, :])
    load(gro, rr.at[0:OWN, :])
    for j in range(4):
        load(src.at[2 * j], ge0.at[j, 0:OWN, :])
        load(src.at[2 * j + 1], go0.at[j, 0:OWN, :])

    def clear():
        for ref in (v0, ge0, ge1, ge2, go0, go1, go2, o10, o11, o12, po, pr, ga, gb, vr):
            for j in range(ref.shape[0]):
                ref[j, OWN:BUF, :] = jnp.zeros((BUF - OWN, ref.shape[2]), F32)
        for ref in (dd, rr, vin):
            ref[OWN:BUF, :] = jnp.zeros((BUF - OWN, ref.shape[1]), F32)

    pl.when(jnp.logical_or(s == 0, s == n_s - 1))(clear)

    barrier = pltpu.get_barrier_semaphore()
    peers = GROUP * 2 * (1 + has_up.astype(jnp.int32) + has_down.astype(jnp.int32)) - 1
    for back in range(2):
        zz = lax.rem(z + nz - back, nz)
        for k in range(GROUP):
            for ds, cond in ((0, None if back else q != k), (1, has_down), (-1, has_up)):
                def greet(zz=zz, k=k, ds=ds):
                    pl.semaphore_signal(barrier, inc=1, device_id={"tm": zz * GROUP + k, "space": s + ds},
                                        device_id_type=MESH)
                when(cond, greet)

    for copy in loads[:6]:
        copy.wait()
    pl.semaphore_wait(barrier, peers)

    def lead(ref, n):
        return lambda r, h: ref.at[0:n, pl.ds(r, h), :]

    def exchange(ref, h, name):
        send_edges(ref, ref, h, SEM[name], SEM[name], t)

    exchange(lead(v0, 4), 1, "v0")
    exchange(rows_of(dd), 4, "dif")
    exchange(rows_of(rr), 4, "gro")
    for copy in loads[6:]:
        copy.wait()
    exchange(lead(ge0, 4), 2, "ge0")
    exchange(lead(go0, 4), 1, "go0")

    lane = lax.broadcasted_iota(jnp.int32, (BUF, LANES), 1)

    def spread(get, c, rows):
        c0 = c * width
        u = get(c0, width)
        west, east = pltpu.roll(u, 1, 1), pltpu.roll(u, width - 1, 1)
        before = pltpu.roll(get(c0 - LANES, LANES), 1, 1) if c > 0 else jnp.zeros((BUF, LANES), F32)
        after = pltpu.roll(get(c0 + width, LANES), LANES - 1, 1) if c < GROUP - 1 else jnp.zeros((BUF, LANES), F32)
        first = jnp.where(lane == 0, before, west[:, :LANES])
        last = jnp.where(lane == LANES - 1, after, east[:, width - LANES:])
        if width > LANES:
            west = jnp.concatenate([first, west[:, LANES:]], axis=1)
            east = jnp.concatenate([east[:, :width - LANES], last], axis=1)
        else:
            west, east = first, last
        north, south = pltpu.roll(u, 1, 0), pltpu.roll(u, BUF - 1, 0)
        u = u[:rows]
        beside = north[:rows] + south[:rows] + west[:rows] + east[:rows]
        n = aa[0:rows, c0:c0 + width] * (beside - 4.0 * u) + bb[0:rows, c0:c0 + width] * u / (1.0 + u * u)
        return n, u

    def cut(c):
        return slice(c * width, (c + 1) * width)

    def field(ref, *lead):
        return lambda c0, w: ref[(*lead, slice(None), slice(c0, c0 + w))]

    def relax(level, j, source, odd_at):
        f = 2.0 ** level
        for c in range(GROUP):
            n, u = spread(source, c, BUF)
            ee[j, :, cut(c)] = u + f * n + ge[level][j, :, cut(c)]
        for c in range(GROUP):
            n, u = spread(field(ee, j), c, BUF)
            ne[j, :, cut(c)] = n
            ob[:, cut(c)] = u + f * n + go[level][j, :, cut(c)]
        for c in range(GROUP):
            n, u = spread(field(ob), c, OWN)
            pair = u + f * n - ee[j, 0:OWN, cut(c)] - 2.0 * f * ne[j, 0:OWN, cut(c)]
            ps[odd_at, :, cut(c)] = pair

    own = slice(0, OWN)

    edges_arrived(rows_of(dd), 4, SEM["dif"])
    edges_arrived(rows_of(rr), 4, SEM["gro"])
    aa[...] = DIFFUSION * dd[...]
    bb[...] = STEP * rr[...]
    edges_arrived(lead(v0, 4), 1, SEM["v0"])

    def first_odd(j):
        for c in range(GROUP):
            n, u = spread(field(v0, j), c, OWN)
            o10[j, own, cut(c)] = u + n + go0[j, own, cut(c)]

    def send_next(source, target, h, name, cond=None):
        send(source(0, OWN), target(0, OWN), SEM[name], SEM[name], following, s)
        send_edges(source, target, h, SEM[name], SEM[name], following)

    first_odd(3)
    send_next(rows_of(o10, 3), rows_of(po, 0), 3, "po0")
    lax.fori_loop(0, 3, lambda j, x: (first_odd(j), x)[1], 0)
    exchange(lead(o10, 3), 3, "o1_0")

    def stage(get, target):
        for k in range(GROUP):
            main = get(k * width, width)
            right = get((k + 1) * width, LANES) if k < GROUP - 1 else jnp.zeros((OWN, LANES), F32)
            left = get(k * width - LANES, LANES) if k > 0 else jnp.zeros((OWN, LANES), F32)
            target[k, :, 0:width] = main
            target[k, :, width:wide] = jnp.where(lane[:OWN] < LANES // 2, right, left)

    def send_group(source, target, h, si, ri, group, itself):
        for k in range(GROUP):
            tm = group * GROUP + k
            me = jnp.logical_and(itself, q == k)

            def keep(k=k):
                pltpu.make_async_copy(source(k)(0, OWN), target(0, OWN), rs.at[ri]).start()
            pl.when(me)(keep)
            send(source(k)(0, OWN), target(0, OWN), si + 3 * k, ri, tm, s, jnp.logical_not(me))
            send_edges(source(k), target, h, si + 3 * k, ri, tm)

    stage(lambda c0, w: ge0[0, own, c0:c0 + w], xa)
    send_group(lambda k: rows_of(xa, k), rows_of(ga, q), 4, SEM["ga"], SEM["ga"] + 3 * q, z, q >= 0)

    edges_arrived(lead(ge0, 4), 2, SEM["ge0"])
    edges_arrived(lead(go0, 4), 1, SEM["go0"])
    edges_arrived(lead(o10, 3), 3, SEM["o1_0"])

    def inner0(j, x):
        relax(0, j + 1, lambda c0, w: o10[j, :, c0:c0 + w], j + 1)
        return x

    lax.fori_loop(0, 3, inner0, 0)
    send_next(rows_of(ps, 3), rows_of(pr, 0), 2, "pr0")
    for c in range(GROUP):
        g = ge0[3, own, cut(c)] + ps[2, :, cut(c)]
        go1[1, own, cut(c)] = g
        o11[1, own, cut(c)] = ee[2, own, cut(c)] + 2.0 * ne[2, own, cut(c)] + g
    send_next(rows_of(o11, 1), rows_of(po, 1), 3, "po1")
    for c in range(GROUP):
        ge1[1, own, cut(c)] = ge0[2, own, cut(c)] + ps[1, :, cut(c)]
    exchange(rows_of(ge1, 1), 2, "ge1")

    all_arrived(rows_of(po, 0), 3, SEM["po0"])
    relax(0, 0, field(po, 0), 0)
    for c in range(GROUP):
        g = ge0[1, own, cut(c)] + ps[0, :, cut(c)]
        go1[0, own, cut(c)] = g
        o11[0, own, cut(c)] = ee[0, own, cut(c)] + 2.0 * ne[0, own, cut(c)] + g
    exchange(rows_of(o11, 0), 3, "o1_1")
    exchange(lead(go1, 2), 1, "go1")

    edges_arrived(rows_of(ge1, 1), 2, SEM["ge1"])
    edges_arrived(rows_of(o11, 0), 3, SEM["o1_1"])
    edges_arrived(lead(go1, 2), 1, SEM["go1"])
    relax(1, 1, field(o11, 0), 5)
    send_next(rows_of(ps, 5), rows_of(pr, 1), 2, "pr1")
    all_arrived(rows_of(pr, 0), 2, SEM["pr0"])
    ge1[0] = ge0[0] + pr[0]
    all_arrived(rows_of(po, 1), 3, SEM["po1"])
    relax(1, 0, field(po, 1), 4)
    for c in range(GROUP):
        g = ge1[1, own, cut(c)] + ps[4, :, cut(c)]
        go2[0, own, cut(c)] = g
        o12[0, own, cut(c)] = ee[0, own, cut(c)] + 4.0 * ne[0, own, cut(c)] + g
    send_next(rows_of(o12, 0), rows_of(po, 2), 3, "po2")
    exchange(rows_of(go2, 0), 2, "go2")

    all_arrived(rows_of(pr, 1), 2, SEM["pr1"])
    ge2[0] = ge1[0] + pr[1]
    edges_arrived(rows_of(go2, 0), 2, SEM["go2"])
    all_arrived(rows_of(po, 2), 3, SEM["po2"])
    relax(2, 0, field(po, 2), 6)

    stage(lambda c0, w: ps[3, :, c0:c0 + w] + ps[5, :, c0:c0 + w] + ps[6, :, c0:c0 + w], xb)
    k_next = lax.rem(following, GROUP)
    z_next = following // GROUP
    send_group(lambda k: rows_of(xb, k), rows_of(gb, k_next), 4, SEM["gb"], SEM["gb"] + 3 * k_next, z_next,
               q < GROUP - 1)

    is_last = t == n_t - 1
    stage(lambda c0, w: ee[0, own, c0:c0 + w], xv)
    for k in range(GROUP):
        tm = lax.rem(following + k, n_t)
        send(xv.at[k], vin.at[0:OWN, :], SEM["old"] + 3 * k, SEM["vin"], tm, s, is_last)
        send_edges(rows_of(xv, k), rows_of(vin), 4, SEM["old"] + 3 * k, SEM["vin"], tm, is_last)

    def own_part(k):
        for whole, part in ((aa, ap), (bb, bp)):
            zero = jnp.zeros((BUF, LANES), F32)
            right = whole[:, (k + 1) * width:(k + 1) * width + LANES] if k < GROUP - 1 else zero
            left = whole[:, k * width - LANES:k * width] if k > 0 else zero
            part[:, 0:width] = whole[:, k * width:(k + 1) * width]
            part[:, width:wide] = jnp.where(lane < LANES // 2, right, left)

    for k in range(GROUP):
        pl.when(q == k)(functools.partial(own_part, k))

    f = 2.0 ** (len(PAIRS))
    all_arrived(rows_of(vin), 4, SEM["vin"])
    for k in range(GROUP):
        all_arrived(rows_of(ga, k), 4, SEM["ga"] + 3 * k)
        all_arrived(rows_of(gb, k), 4, SEM["gb"] + 3 * k)
        u = vin[...] if k == 0 else vo[k - 1]
        beside = pltpu.roll(u, 1, 0) + pltpu.roll(u, BUF - 1, 0) + pltpu.roll(u, 1, 1) + pltpu.roll(u, wide - 1, 1)
        n = ap[...] * (beside - 4.0 * u) + bp[...] * u / (1.0 + u * u)
        vo[k] = u + f * n + (ga[k] + gb[k])
        if k == GROUP - 1:
            ongoing = z < nz - 1
            tm = lax.rem(t + GROUP, n_t)
            send(vo.at[k, 0:OWN, :], vin.at[0:OWN, :], SEM["vin"], SEM["vin"], tm, s, ongoing)
            send_edges(rows_of(vo, k), rows_of(vin), 4, SEM["vin"], SEM["vin"], tm, ongoing)

        def block(r, h, k=k):
            return vo.at[k, pl.ds(r, h), 0:width]

        def place(r, h):
            return vr.at[q, pl.ds(r, h), :]

        tm = z * GROUP + k
        me = q == k

        def keep(k=k):
            pltpu.make_async_copy(block(0, OWN), place(0, OWN), rs.at[SEM["vr"] + 3 * q]).start()
        pl.when(me)(keep)
        send(block(0, OWN), place(0, OWN), SEM["vr"] + 3 * k, SEM["vr"] + 3 * q, tm, s, jnp.logical_not(me))
        send_edges(block, place, 4, SEM["vr"] + 3 * k, SEM["vr"] + 3 * q, tm)

    for k in range(GROUP):
        all_arrived(rows_of(vr, k), 4, SEM["vr"] + 3 * k)
    for c in range(GROUP):
        n, u = spread(lambda c0, w: vr[c0 // width, :, c0 % width:c0 % width + w], c, BUF)
        res[0, :, cut(c)] = u[:OWN]
        res[1, :, cut(c)] = (u + n + go0[0, :, cut(c)])[:OWN]
        ee[1, :, cut(c)] = u + 2.0 * n + go1[0, :, cut(c)]
        ee[2, :, cut(c)] = u + 4.0 * n + go2[0, :, cut(c)]
    stores = []

    def store(j):
        copy = pltpu.make_async_copy(res.at[j], out.at[j], ls.at[j])
        copy.start()
        stores.append(copy)

    store(0)
    store(1)
    for c in range(GROUP):
        n, u = spread(field(ee, 2), c, BUF)
        res[4, :, cut(c)] = u[:OWN]
        res[5, :, cut(c)] = (u + n + go0[2, :, cut(c)])[:OWN]
        ee[3, :, cut(c)] = u + 2.0 * n + go1[1, :, cut(c)]
    store(4)
    store(5)
    for j in (1, 3):
        for c in range(GROUP):
            n, u = spread(field(ee, j), c, OWN)
            res[2 * j, :, cut(c)] = u
            res[2 * j + 1, :, cut(c)] = u + n + go0[j, own, cut(c)]
        store(2 * j)
        store(2 * j + 1)
    for copy in stores:
        copy.wait()
    for cond, copy in sent:
        when(cond, lambda copy=copy: copy().wait_send())


def solution(mesh):
    n_t, n_s = mesh.shape["tm"], mesh.shape["space"]

    def body(initial, source, diffusivity, growth):
        cols = initial.shape[2]
        wide = cols // GROUP + LANES

        def full(*n):
            return pltpu.VMEM((*n, BUF, cols), F32)

        def part(*n):
            return pltpu.VMEM((*n, BUF, wide), F32)

        scratch = [
            full(4), full(4), full(2), full(1), full(4), full(2), full(1), full(4), full(2), full(1),
            full(3), full(2), full(4), full(4), full(), pltpu.VMEM((7, OWN, cols), F32),
            full(), full(), full(), full(),
            pltpu.VMEM((GROUP, OWN, wide), F32), pltpu.VMEM((GROUP, OWN, wide), F32), pltpu.VMEM((GROUP, OWN, wide), F32),
            part(GROUP), part(GROUP), part(), part(GROUP), part(), part(),
            pltpu.VMEM((GROUP, BUF, cols // GROUP), F32),
            pltpu.VMEM(initial.shape, F32),
            pltpu.SemaphoreType.DMA((N_SEM,)), pltpu.SemaphoreType.DMA((N_SEM,)), pltpu.SemaphoreType.DMA((14,)),
        ]
        return pl.pallas_call(
            functools.partial(kernel, n_t, n_s, cols),
            out_shape=jax.ShapeDtypeStruct(initial.shape, F32),
            in_specs=[pl.BlockSpec(memory_space=pl.ANY)] * 4,
            out_specs=pl.BlockSpec(memory_space=pl.ANY),
            scratch_shapes=scratch,
            compiler_params=pltpu.CompilerParams(collective_id=0, has_side_effects=True),
        )(initial, source, diffusivity, growth)

    placed = (P("tm", "space", None), P("tm", "space", None), P("space", None), P("space", None))
    return jax.shard_map(body, mesh=mesh, in_specs=placed, out_specs=P("tm", "space", None), check_vma=False)
```

```python
import functools

import jax
import jax.numpy as jnp
from jax import lax
from jax.experimental import pallas as pl
from jax.experimental.pallas import tpu as pltpu
from jax.sharding import PartitionSpec as P

MESH = pl.DeviceIdType.MESH
F32 = jnp.float32
DIFFUSION = 0.03
STEP = 0.02

OWN = 16
BUF = 24
DEEP = 32
LANES = 128
CUTS = 4
GROUP = 8
PAIRS = (4, 2, 1)

_names = [
    ("v0", 3), ("dif", 3), ("gro", 3), ("ge0", 3), ("go0", 3), ("dif2", 3), ("gro2", 3), ("pv", 3), ("pg", 3),
    ("o1_0", 3), ("o1_1", 3), ("ge1", 3), ("go1", 3), ("go2", 3),
    ("po1", 3), ("po2", 3), ("pr0", 3), ("pr1", 3),
    ("ga", 24), ("gb", 24), ("vin", 3), ("vr", 24), ("old", 24),
]
SEM = {}
_at = 0
for _name, _count in _names:
    SEM[_name] = _at
    _at += _count
N_SEM = _at


def kernel(n_t, n_s, cols, ini, src, dif, gro, out, v0, ge0, ge1, ge2, go0, go1, go2, o10, o11, o12,
           po, pr, pv, pg, ee, ne, ob, ps, dd, rr, aa, bb, xa, xb, ga, gb, vin, vo, ap, bp, vr, res,
           ss, rs, ls):
    ge, go, o1 = (ge0, ge1, ge2), (go0, go1, go2), (o10, o11, o12)
    span = cols // CUTS
    width = cols // GROUP
    wide = width + LANES
    t, s = lax.axis_index("tm"), lax.axis_index("space")
    z, q = t // GROUP, lax.rem(t, GROUP)

    def holder(group, block):
        return group * GROUP + lax.rem(block + group * (GROUP // 2), GROUP)

    mine = lax.rem(q + z * (GROUP // 2), GROUP)
    following = lax.rem(t + 1, n_t)
    has_up, has_down = s > 0, s < n_s - 1
    sent = []

    def when(cond, fn):
        if cond is None:
            fn()
        else:
            pl.when(cond)(fn)

    def both(a, b):
        return b if a is None else (a if b is None else jnp.logical_and(a, b))

    def send(source, target, si, ri, tm, space, cond=None):
        def copy():
            return pltpu.make_async_remote_copy(
                src_ref=source, dst_ref=target, send_sem=ss.at[si], recv_sem=rs.at[ri],
                device_id={"tm": tm, "space": space}, device_id_type=MESH)
        when(cond, lambda: copy().start())
        sent.append((cond, copy))

    def send_edges(source, target, h, si, ri, tm, cond=None, total=BUF):
        send(source(OWN - h, h), target(total - h, h), si + 1, ri + 1, tm, s + 1, both(cond, has_down))
        send(source(0, h), target(OWN, h), si + 2, ri + 2, tm, s - 1, both(cond, has_up))

    def arrived(target, ri, cond=None):
        def wait():
            pltpu.make_async_remote_copy(
                src_ref=target, dst_ref=target, send_sem=ss.at[0], recv_sem=rs.at[ri],
                device_id={"tm": following, "space": s}, device_id_type=MESH).wait_recv()
        when(cond, wait)

    def edges_arrived(target, h, ri, total=BUF):
        arrived(target(total - h, h), ri + 1, has_up)
        arrived(target(OWN, h), ri + 2, has_down)

    def all_arrived(target, h, ri, total=BUF):
        arrived(target(0, OWN), ri)
        edges_arrived(target, h, ri, total)

    def rows_of(ref, *lead):
        return lambda r, h: ref.at[(*lead, pl.ds(r, h), slice(None))]

    loads = []

    def load(source, target):
        copy = pltpu.make_async_copy(source, target, ls.at[len(loads)])
        copy.start()
        loads.append(copy)

    for j in range(4):
        load(ini.at[2 * j], v0.at[j, 0:OWN, :])
    load(dif, dd.at[0:OWN, :])
    load(gro, rr.at[0:OWN, :])
    for j in range(4):
        load(src.at[2 * j], ge0.at[j, 0:OWN, :])
        load(src.at[2 * j + 1], go0.at[j, 0:OWN, :])

    def clear():
        for ref in (v0, ge0, ge1, ge2, go0, go1, go2, o10, o11, o12, po, pr, ga, gb, vr):
            for j in range(ref.shape[0]):
                ref[j, OWN:, :] = jnp.zeros((ref.shape[1] - OWN, ref.shape[2]), F32)
        for ref in (dd, rr, pv, pg, vin):
            ref[OWN:, :] = jnp.zeros((ref.shape[0] - OWN, ref.shape[1]), F32)

    pl.when(jnp.logical_or(s == 0, s == n_s - 1))(clear)

    barrier = pltpu.get_barrier_semaphore()
    last = q // (GROUP - 1)
    peers = (GROUP + GROUP * last + (1 - z) * (1 - last)) * (
        1 + has_up.astype(jnp.int32) + has_down.astype(jnp.int32)) - 1

    def greet(tm, cond_here=None, cond=None):
        for ds, there in ((0, cond_here), (1, has_down), (-1, has_up)):
            when(both(cond, there), lambda ds=ds: pl.semaphore_signal(
                barrier, inc=1, device_id={"tm": tm, "space": s + ds}, device_id_type=MESH))

    greet(lax.rem(z * GROUP + n_t - 1, n_t))
    greet(mine, None, jnp.logical_and(z == 1, mine < GROUP - 1))
    for k in range(GROUP):
        greet(z * GROUP + k, q != k)

    for copy in loads[:6]:
        copy.wait()
    pl.semaphore_wait(barrier, peers)

    def lead(ref, n):
        return lambda r, h: ref.at[0:n, pl.ds(r, h), :]

    def exchange(ref, h, name):
        send_edges(ref, ref, h, SEM[name], SEM[name], t)

    def send_next(source, target, h, name):
        send_edges(source, target, h, SEM[name], SEM[name], following)
        send(source(0, OWN), target(0, OWN), SEM[name], SEM[name], following, s)

    exchange(lead(v0, 3), 1, "v0")
    send_next(rows_of(v0, 3), rows_of(pv), 4, "pv")
    for copy in loads[6:]:
        copy.wait()
    send_next(rows_of(go0, 3), rows_of(pg), 3, "pg")
    send_edges(rows_of(dd), rows_of(dd), 4, SEM["dif"], SEM["dif"], t, None, DEEP)
    send_edges(rows_of(rr), rows_of(rr), 4, SEM["gro"], SEM["gro"], t, None, DEEP)

    lane = lax.broadcasted_iota(jnp.int32, (BUF, LANES), 1)

    def spread(get, c, rows):
        c0 = c * span
        u = get(c0, span)
        west, east = pltpu.roll(u, 1, 1), pltpu.roll(u, span - 1, 1)
        before = pltpu.roll(get(c0 - LANES, LANES), 1, 1) if c > 0 else jnp.zeros((BUF, LANES), F32)
        after = pltpu.roll(get(c0 + span, LANES), LANES - 1, 1) if c < CUTS - 1 else jnp.zeros((BUF, LANES), F32)
        first = jnp.where(lane == 0, before, west[:, :LANES])
        last = jnp.where(lane == LANES - 1, after, east[:, span - LANES:])
        if span > LANES:
            west = jnp.concatenate([first, west[:, LANES:]], axis=1)
            east = jnp.concatenate([east[:, :span - LANES], last], axis=1)
        else:
            west, east = first, last
        north, south = pltpu.roll(u, 1, 0), pltpu.roll(u, BUF - 1, 0)
        u = u[:rows]
        beside = north[:rows] + south[:rows] + west[:rows] + east[:rows]
        n = aa[0:rows, c0:c0 + span] * (beside - 4.0 * u) + bb[0:rows, c0:c0 + span] * u / (1.0 + u * u)
        return n, u

    def cut(c):
        return slice(c * span, (c + 1) * span)

    def field(ref, *lead):
        return lambda c0, w: ref[(*lead, slice(None), slice(c0, c0 + w))]

    def relax(level, j, source, odd_at):
        f = 2.0 ** level
        for c in range(CUTS):
            n, u = spread(source, c, BUF)
            ee[j, :, cut(c)] = u + f * n + ge[level][j, :, cut(c)]
        for c in range(CUTS):
            n, u = spread(field(ee, j), c, BUF)
            ne[j, :, cut(c)] = n
            ob[:, cut(c)] = u + f * n + go[level][j, :, cut(c)]
        for c in range(CUTS):
            n, u = spread(field(ob), c, OWN)
            pair = u + f * n - ee[j, 0:OWN, cut(c)] - 2.0 * f * ne[j, 0:OWN, cut(c)]
            ps[odd_at, :, cut(c)] = pair

    own = slice(0, OWN)

    edges_arrived(lead(v0, 3), 1, SEM["v0"])
    aa[own] = DIFFUSION * dd[own]
    bb[own] = STEP * rr[own]

    def first_odd(j):
        for c in range(CUTS):
            n, u = spread(field(v0, j), c, OWN)
            o10[j, own, cut(c)] = u + n + go0[j, own, cut(c)]

    lax.fori_loop(0, 3, lambda j, x: (first_odd(j), x)[1], 0)
    exchange(lead(o10, 3), 3, "o1_0")
    exchange(lead(ge0, 4), 2, "ge0")
    exchange(lead(go0, 4), 1, "go0")
    for ref, name in ((dd, "dif2"), (rr, "gro2")):
        send(ref.at[8:12, :], ref.at[24:28, :], SEM[name] + 1, SEM[name] + 1, t, s + 1, has_down)
        send(ref.at[4:8, :], ref.at[20:24, :], SEM[name] + 2, SEM[name] + 2, t, s - 1, has_up)

    def stage(get, target):
        for k in range(GROUP):
            main = get(k * width, width)
            right = get((k + 1) * width, LANES) if k < GROUP - 1 else jnp.zeros((OWN, LANES), F32)
            left = get(k * width - LANES, LANES) if k > 0 else jnp.zeros((OWN, LANES), F32)
            target[k, :, 0:width] = main
            target[k, :, width:wide] = jnp.where(lane[:OWN] < LANES // 2, right, left)

    def send_group(source, target, si, ri, group, itself, cond=None):
        for k in range(GROUP):
            tm = holder(group, k)
            me = jnp.logical_and(itself, mine == k)

            def keep(k=k):
                pltpu.make_async_copy(source(k)(0, OWN), target(0, OWN), rs.at[ri]).start()
            pl.when(me)(keep)
            send_edges(source(k), target, 8, si + 3 * k, ri, tm, cond, DEEP)
            send(source(k)(0, OWN), target(0, OWN), si + 3 * k, ri, tm, s, both(cond, jnp.logical_not(me)))

    edges_arrived(rows_of(dd), 4, SEM["dif"], DEEP)
    edges_arrived(rows_of(rr), 4, SEM["gro"], DEEP)
    for r, at in ((OWN, OWN), (BUF - 4, DEEP - 4)):
        aa[r:r + 4] = DIFFUSION * dd[at:at + 4]
        bb[r:r + 4] = STEP * rr[at:at + 4]
    edges_arrived(lead(o10, 3), 3, SEM["o1_0"])
    edges_arrived(lead(ge0, 4), 2, SEM["ge0"])
    edges_arrived(lead(go0, 4), 1, SEM["go0"])

    relax(0, 2, field(o10, 1), 2)
    for c in range(CUTS):
        g = ge0[3, own, cut(c)] + ps[2, :, cut(c)]
        go1[1, own, cut(c)] = g
        o11[1, own, cut(c)] = ee[2, own, cut(c)] + 2.0 * ne[2, own, cut(c)] + g
    send_next(rows_of(o11, 1), rows_of(po, 1), 3, "po1")
    relax(0, 3, field(o10, 2), 3)
    send_next(rows_of(ps, 3), rows_of(pr, 0), 2, "pr0")
    relax(0, 1, field(o10, 0), 1)
    for c in range(CUTS):
        ge1[1, own, cut(c)] = ge0[2, own, cut(c)] + ps[1, :, cut(c)]
    exchange(rows_of(ge1, 1), 2, "ge1")

    all_arrived(rows_of(pv), 4, SEM["pv"])
    all_arrived(rows_of(pg), 3, SEM["pg"])
    for c in range(CUTS):
        n, u = spread(field(pv), c, BUF)
        po[0, :, cut(c)] = u + n + pg[:, cut(c)]
    relax(0, 0, field(po, 0), 0)
    for c in range(CUTS):
        g = ge0[1, own, cut(c)] + ps[0, :, cut(c)]
        go1[0, own, cut(c)] = g
        o11[0, own, cut(c)] = ee[0, own, cut(c)] + 2.0 * ne[0, own, cut(c)] + g
    exchange(rows_of(o11, 0), 3, "o1_1")
    exchange(lead(go1, 2), 1, "go1")
    stage(lambda c0, w: ge0[0, own, c0:c0 + w], xa)
    send_group(lambda k: rows_of(xa, k), rows_of(ga, q), SEM["ga"], SEM["ga"] + 3 * q, z, q >= 0)

    edges_arrived(rows_of(ge1, 1), 2, SEM["ge1"])
    edges_arrived(rows_of(o11, 0), 3, SEM["o1_1"])
    edges_arrived(lead(go1, 2), 1, SEM["go1"])
    relax(1, 1, field(o11, 0), 5)
    send_next(rows_of(ps, 5), rows_of(pr, 1), 2, "pr1")
    all_arrived(rows_of(pr, 0), 2, SEM["pr0"])
    ge1[0] = ge0[0] + pr[0]
    all_arrived(rows_of(po, 1), 3, SEM["po1"])
    relax(1, 0, field(po, 1), 4)
    for c in range(CUTS):
        g = ge1[1, own, cut(c)] + ps[4, :, cut(c)]
        go2[0, own, cut(c)] = g
        o12[0, own, cut(c)] = ee[0, own, cut(c)] + 4.0 * ne[0, own, cut(c)] + g
    send_next(rows_of(o12, 0), rows_of(po, 2), 3, "po2")
    exchange(rows_of(go2, 0), 2, "go2")

    all_arrived(rows_of(pr, 1), 2, SEM["pr1"])
    ge2[0] = ge1[0] + pr[1]
    edges_arrived(rows_of(go2, 0), 2, SEM["go2"])
    all_arrived(rows_of(po, 2), 3, SEM["po2"])
    relax(2, 0, field(po, 2), 6)

    is_last = t == n_t - 1

    def onward(c0, w):
        at = slice(c0, c0 + w)
        pairs = ps[3, :, at] + ps[5, :, at] + ps[6, :, at]
        return pairs + jnp.where(is_last, ee[0, own, at] + 8.0 * ne[0, own, at], 0.0)

    stage(onward, xb)
    for k in range(GROUP):
        tm = lax.rem(following + k, n_t)
        send_edges(rows_of(xb, k), rows_of(vin), 8, SEM["old"] + 3 * k, SEM["vin"], tm, is_last, DEEP)
        send(xb.at[k], vin.at[0:OWN, :], SEM["old"] + 3 * k, SEM["vin"], tm, s, is_last)
    k_next = lax.rem(following, GROUP)
    z_next = following // GROUP
    send_group(lambda k: rows_of(xb, k), rows_of(gb, k_next), SEM["gb"], SEM["gb"] + 3 * k_next, z_next,
               q < GROUP - 1, jnp.logical_not(is_last))

    for ref, name in ((dd, "dif2"), (rr, "gro2")):
        arrived(ref.at[24:28, :], SEM[name] + 1, has_up)
        arrived(ref.at[20:24, :], SEM[name] + 2, has_down)
    lane_deep = lax.broadcasted_iota(jnp.int32, (DEEP, LANES), 1)

    def own_part(k):
        for whole, part, scale in ((dd, ap, DIFFUSION), (rr, bp, STEP)):
            zero = jnp.zeros((DEEP, LANES), F32)
            right = whole[:, (k + 1) * width:(k + 1) * width + LANES] if k < GROUP - 1 else zero
            left = whole[:, k * width - LANES:k * width] if k > 0 else zero
            part[:, 0:width] = scale * whole[:, k * width:(k + 1) * width]
            part[:, width:wide] = scale * jnp.where(lane_deep < LANES // 2, right, left)

    for k in range(GROUP):
        pl.when(mine == k)(functools.partial(own_part, k))

    f = 2.0 ** (len(PAIRS))
    all_arrived(rows_of(vin), 8, SEM["vin"], DEEP)
    for k in range(GROUP):
        all_arrived(rows_of(ga, k), 8, SEM["ga"] + 3 * k, DEEP)
        if k == 0:
            arrived(gb.at[0, 0:OWN, :], SEM["gb"], z == 1)
            arrived(gb.at[0, DEEP - 8:DEEP, :], SEM["gb"] + 1, jnp.logical_and(z == 1, has_up))
            arrived(gb.at[0, OWN:OWN + 8, :], SEM["gb"] + 2, jnp.logical_and(z == 1, has_down))
        else:
            all_arrived(rows_of(gb, k), 8, SEM["gb"] + 3 * k, DEEP)
        u = vin[...] if k == 0 else vo[k - 1]
        beside = pltpu.roll(u, 1, 0) + pltpu.roll(u, DEEP - 1, 0) + pltpu.roll(u, 1, 1) + pltpu.roll(u, wide - 1, 1)
        n = ap[...] * (beside - 4.0 * u) + bp[...] * u / (1.0 + u * u)
        u = u + f * n + gb[k]
        if k == 0:
            u = jnp.where(z == 0, vin[...], u)
        vo[k] = u + ga[k]
        if k == GROUP - 1:
            tm = holder(1, mine)
            send_edges(rows_of(vo, k), rows_of(vin), 8, SEM["vin"], SEM["vin"], tm, z == 0, DEEP)
            send(vo.at[k, 0:OWN, :], vin.at[0:OWN, :], SEM["vin"], SEM["vin"], tm, s, z == 0)

        def block(r, h, k=k):
            return vo.at[k, pl.ds(r, h), 0:width]

        place = rows_of(vr, mine)
        tm = z * GROUP + k
        me = q == k

        def keep():
            pltpu.make_async_copy(block(0, OWN), place(0, OWN), rs.at[SEM["vr"] + 3 * mine]).start()
        pl.when(me)(keep)
        send_edges(block, place, 4, SEM["vr"] + 3 * k, SEM["vr"] + 3 * mine, tm)
        send(block(0, OWN), place(0, OWN), SEM["vr"] + 3 * k, SEM["vr"] + 3 * mine, tm, s, jnp.logical_not(me))

    for k in range(GROUP):
        all_arrived(rows_of(vr, k), 4, SEM["vr"] + 3 * k)

    def returned(c0, w):
        if w <= width:
            return vr[c0 // width, :, c0 % width:c0 % width + w]
        return jnp.concatenate([vr[c0 // width + i] for i in range(w // width)], axis=1)

    for c in range(CUTS):
        n, u = spread(returned, c, BUF)
        res[0, :, cut(c)] = u[:OWN]
        res[1, :, cut(c)] = (u + n + go0[0, :, cut(c)])[:OWN]
        ee[1, :, cut(c)] = u + 2.0 * n + go1[0, :, cut(c)]
        ee[2, :, cut(c)] = u + 4.0 * n + go2[0, :, cut(c)]
    stores = []

    def store(j):
        copy = pltpu.make_async_copy(res.at[j], out.at[j], ls.at[j])
        copy.start()
        stores.append(copy)

    store(0)
    store(1)
    for c in range(CUTS):
        n, u = spread(field(ee, 2), c, BUF)
        res[4, :, cut(c)] = u[:OWN]
        res[5, :, cut(c)] = (u + n + go0[2, :, cut(c)])[:OWN]
        ee[3, :, cut(c)] = u + 2.0 * n + go1[1, :, cut(c)]
    store(4)
    store(5)
    for j in (1, 3):
        for c in range(CUTS):
            n, u = spread(field(ee, j), c, OWN)
            res[2 * j, :, cut(c)] = u
            res[2 * j + 1, :, cut(c)] = u + n + go0[j, own, cut(c)]
        store(2 * j)
        store(2 * j + 1)
    for copy in stores:
        copy.wait()
    for cond, copy in sent:
        when(cond, lambda copy=copy: copy().wait_send())


def solution(mesh):
    n_t, n_s = mesh.shape["tm"], mesh.shape["space"]

    def body(initial, source, diffusivity, growth):
        cols = initial.shape[2]
        wide = cols // GROUP + LANES

        def full(*n):
            return pltpu.VMEM((*n, BUF, cols), F32)

        def part(*n):
            return pltpu.VMEM((*n, DEEP, wide), F32)

        scratch = [
            full(4), full(4), full(2), full(1), full(4), full(2), full(1), full(4), full(2), full(1),
            full(3), full(2), full(), full(), full(4), full(4), full(), pltpu.VMEM((7, OWN, cols), F32),
            pltpu.VMEM((DEEP, cols), F32), pltpu.VMEM((DEEP, cols), F32), full(), full(),
            pltpu.VMEM((GROUP, OWN, wide), F32), pltpu.VMEM((GROUP, OWN, wide), F32),
            part(GROUP), part(GROUP), part(), part(GROUP), part(), part(),
            pltpu.VMEM((GROUP, BUF, cols // GROUP), F32),
            pltpu.VMEM(initial.shape, F32),
            pltpu.SemaphoreType.DMA((N_SEM,)), pltpu.SemaphoreType.DMA((N_SEM,)), pltpu.SemaphoreType.DMA((14,)),
        ]
        return pl.pallas_call(
            functools.partial(kernel, n_t, n_s, cols),
            out_shape=jax.ShapeDtypeStruct(initial.shape, F32),
            in_specs=[pl.BlockSpec(memory_space=pl.ANY)] * 4,
            out_specs=pl.BlockSpec(memory_space=pl.ANY),
            scratch_shapes=scratch,
            compiler_params=pltpu.CompilerParams(collective_id=0, has_side_effects=True),
        )(initial, source, diffusivity, growth)

    placed = (P("tm", "space", None), P("tm", "space", None), P("space", None), P("space", None))
    return jax.shard_map(body, mesh=mesh, in_specs=placed, out_specs=P("tm", "space", None), check_vma=False)
```

```python
import functools

import jax
import jax.numpy as jnp
from jax import lax
from jax.experimental import pallas as pl
from jax.experimental.pallas import tpu as pltpu
from jax.sharding import PartitionSpec as P

MESH = pl.DeviceIdType.MESH
F32 = jnp.float32
DIFFUSION = 0.03
STEP = 0.02

OWN = 16
BUF = 24
DEEP = 32
LANES = 128
CUTS = 4
GROUP = 8
PAIRS = (4, 2, 1)

_names = [
    ("v0", 3), ("dif", 3), ("gro", 3), ("ge0", 3), ("go0", 3), ("dif2", 3), ("gro2", 3), ("pv", 3), ("pg", 3),
    ("o1_0", 3), ("o1_1", 3), ("ge1", 3), ("go1", 3), ("go2", 3),
    ("po1", 3), ("po2", 3), ("pr0", 3), ("pr1", 3),
    ("ga", 24), ("gae", 3), ("gb", 24), ("vin", 3), ("vr", 24), ("old", 24),
]
SEM = {}
_at = 0
for _name, _count in _names:
    SEM[_name] = _at
    _at += _count
N_SEM = _at


def kernel(n_t, n_s, cols, ini, src, dif, gro, out, v0, ge0, ge1, ge2, go0, go1, go2, o10, o11, o12,
           po, pr, pv, pg, ee, ne, ob, ps, dd, rr, aa, bb, xa, xb, ga, gb, vin, vo, ap, bp, vr, res,
           ss, rs, ls):
    ge, go, o1 = (ge0, ge1, ge2), (go0, go1, go2), (o10, o11, o12)
    span = cols // CUTS
    width = cols // GROUP
    wide = width + LANES
    t, s = lax.axis_index("tm"), lax.axis_index("space")
    z, q = t // GROUP, lax.rem(t, GROUP)

    def holder(group, block):
        return group * GROUP + lax.rem(block + group * (GROUP // 2), GROUP)

    mine = lax.rem(q + z * (GROUP // 2), GROUP)
    following = lax.rem(t + 1, n_t)
    has_up, has_down = s > 0, s < n_s - 1
    sent = []

    def when(cond, fn):
        if cond is None:
            fn()
        else:
            pl.when(cond)(fn)

    def both(a, b):
        return b if a is None else (a if b is None else jnp.logical_and(a, b))

    def send(source, target, si, ri, tm, space, cond=None):
        def copy():
            return pltpu.make_async_remote_copy(
                src_ref=source, dst_ref=target, send_sem=ss.at[si], recv_sem=rs.at[ri],
                device_id={"tm": tm, "space": space}, device_id_type=MESH)
        when(cond, lambda: copy().start())
        sent.append((cond, copy))

    def settle():
        for cond, copy in sent:
            when(cond, lambda copy=copy: copy().wait_send())
        sent.clear()

    def send_edges(source, target, h, si, ri, tm, cond=None, total=BUF):
        send(source(OWN - h, h), target(total - h, h), si + 1, ri + 1, tm, s + 1, both(cond, has_down))
        send(source(0, h), target(OWN, h), si + 2, ri + 2, tm, s - 1, both(cond, has_up))

    def arrived(target, ri, cond=None):
        def wait():
            pltpu.make_async_remote_copy(
                src_ref=target, dst_ref=target, send_sem=ss.at[0], recv_sem=rs.at[ri],
                device_id={"tm": following, "space": s}, device_id_type=MESH).wait_recv()
        when(cond, wait)

    def edges_arrived(target, h, ri, total=BUF):
        arrived(target(total - h, h), ri + 1, has_up)
        arrived(target(OWN, h), ri + 2, has_down)

    def all_arrived(target, h, ri, total=BUF):
        arrived(target(0, OWN), ri)
        edges_arrived(target, h, ri, total)

    def rows_of(ref, *lead):
        return lambda r, h: ref.at[(*lead, pl.ds(r, h), slice(None))]

    loads = []

    def load(source, target):
        copy = pltpu.make_async_copy(source, target, ls.at[len(loads)])
        copy.start()
        loads.append(copy)

    for j in range(4):
        load(ini.at[2 * j], v0.at[j, 0:OWN, :])
    load(dif, dd.at[0:OWN, :])
    load(gro, rr.at[0:OWN, :])
    for j in range(4):
        load(src.at[2 * j], ge0.at[j, 0:OWN, :])
        load(src.at[2 * j + 1], go0.at[j, 0:OWN, :])

    def clear():
        for ref in (v0, ge0, ge1, ge2, go0, go1, go2, o10, o11, o12, po, pr, ga, gb, vr):
            for j in range(ref.shape[0]):
                ref[j, OWN:, :] = jnp.zeros((ref.shape[1] - OWN, ref.shape[2]), F32)
        for ref in (dd, rr, pv, pg, vin):
            ref[OWN:, :] = jnp.zeros((ref.shape[0] - OWN, ref.shape[1]), F32)

    pl.when(jnp.logical_or(s == 0, s == n_s - 1))(clear)

    barrier = pltpu.get_barrier_semaphore()
    last = q // (GROUP - 1)
    peers = (GROUP + GROUP * last + (1 - z) * (1 - last)) * (
        1 + has_up.astype(jnp.int32) + has_down.astype(jnp.int32)) - 1

    def greet(tm, cond_here=None, cond=None):
        for ds, there in ((0, cond_here), (1, has_down), (-1, has_up)):
            when(both(cond, there), lambda ds=ds: pl.semaphore_signal(
                barrier, inc=1, device_id={"tm": tm, "space": s + ds}, device_id_type=MESH))

    greet(lax.rem(z * GROUP + n_t - 1, n_t))
    greet(mine, None, jnp.logical_and(z == 1, mine < GROUP - 1))
    for k in range(GROUP):
        greet(z * GROUP + k, q != k)

    for copy in loads[:6]:
        copy.wait()
    pl.semaphore_wait(barrier, peers)

    def lead(ref, n):
        return lambda r, h: ref.at[0:n, pl.ds(r, h), :]

    def exchange(ref, h, name):
        send_edges(ref, ref, h, SEM[name], SEM[name], t)

    def send_next(source, target, h, name):
        send_edges(source, target, h, SEM[name], SEM[name], following)
        send(source(0, OWN), target(0, OWN), SEM[name], SEM[name], following, s)

    exchange(lead(v0, 3), 1, "v0")
    send_next(rows_of(v0, 3), rows_of(pv), 4, "pv")
    for copy in loads[6:]:
        copy.wait()
    send_next(rows_of(go0, 3), rows_of(pg), 3, "pg")
    send_edges(rows_of(dd), rows_of(dd), 4, SEM["dif"], SEM["dif"], t, None, DEEP)
    send_edges(rows_of(rr), rows_of(rr), 4, SEM["gro"], SEM["gro"], t, None, DEEP)

    lane = lax.broadcasted_iota(jnp.int32, (BUF, LANES), 1)

    def spread(get, c, rows):
        c0 = c * span
        u = get(c0, span)
        west, east = pltpu.roll(u, 1, 1), pltpu.roll(u, span - 1, 1)
        before = pltpu.roll(get(c0 - LANES, LANES), 1, 1) if c > 0 else jnp.zeros((BUF, LANES), F32)
        after = pltpu.roll(get(c0 + span, LANES), LANES - 1, 1) if c < CUTS - 1 else jnp.zeros((BUF, LANES), F32)
        first = jnp.where(lane == 0, before, west[:, :LANES])
        last = jnp.where(lane == LANES - 1, after, east[:, span - LANES:])
        if span > LANES:
            west = jnp.concatenate([first, west[:, LANES:]], axis=1)
            east = jnp.concatenate([east[:, :span - LANES], last], axis=1)
        else:
            west, east = first, last
        north, south = pltpu.roll(u, 1, 0), pltpu.roll(u, BUF - 1, 0)
        u = u[:rows]
        beside = north[:rows] + south[:rows] + west[:rows] + east[:rows]
        n = aa[0:rows, c0:c0 + span] * (beside - 4.0 * u) + bb[0:rows, c0:c0 + span] * u / (1.0 + u * u)
        return n, u

    def cut(c):
        return slice(c * span, (c + 1) * span)

    def field(ref, *lead):
        return lambda c0, w: ref[(*lead, slice(None), slice(c0, c0 + w))]

    def relax(level, j, source, odd_at):
        f = 2.0 ** level
        for c in range(CUTS):
            n, u = spread(source, c, BUF)
            ee[j, :, cut(c)] = u + f * n + ge[level][j, :, cut(c)]
        for c in range(CUTS):
            n, u = spread(field(ee, j), c, BUF)
            ne[j, :, cut(c)] = n
            ob[:, cut(c)] = u + f * n + go[level][j, :, cut(c)]
        for c in range(CUTS):
            n, u = spread(field(ob), c, OWN)
            pair = u + f * n - ee[j, 0:OWN, cut(c)] - 2.0 * f * ne[j, 0:OWN, cut(c)]
            ps[odd_at, :, cut(c)] = pair

    own = slice(0, OWN)

    edges_arrived(lead(v0, 3), 1, SEM["v0"])
    aa[own] = DIFFUSION * dd[own]
    bb[own] = STEP * rr[own]

    def first_odd(j):
        for c in range(CUTS):
            n, u = spread(field(v0, j), c, OWN)
            o10[j, own, cut(c)] = u + n + go0[j, own, cut(c)]

    lax.fori_loop(0, 3, lambda j, x: (first_odd(j), x)[1], 0)
    exchange(lead(o10, 3), 3, "o1_0")
    exchange(lead(ge0, 4), 2, "ge0")
    exchange(lead(go0, 4), 1, "go0")

    def stage(get, target):
        for k in range(GROUP):
            main = get(k * width, width)
            right = get((k + 1) * width, LANES) if k < GROUP - 1 else jnp.zeros((OWN, LANES), F32)
            left = get(k * width - LANES, LANES) if k > 0 else jnp.zeros((OWN, LANES), F32)
            target[k, :, 0:width] = main
            target[k, :, width:wide] = jnp.where(lane[:OWN] < LANES // 2, right, left)

    def send_group(source, target, si, ri, group, itself, cond=None, edges=True):
        for k in range(GROUP):
            tm = holder(group, k)
            me = jnp.logical_and(itself, mine == k)

            def keep(k=k):
                pltpu.make_async_copy(source(k)(0, OWN), target(0, OWN), rs.at[ri]).start()
            pl.when(me)(keep)
            if edges:
                send_edges(source(k), target, 8, si + 3 * k, ri, tm, cond, DEEP)
            send(source(k)(0, OWN), target(0, OWN), si + 3 * k, ri, tm, s, both(cond, jnp.logical_not(me)))

    stage(lambda c0, w: ge0[0, own, c0:c0 + w], xa)
    send_group(lambda k: rows_of(xa, k), rows_of(ga, q), SEM["ga"], SEM["ga"] + 3 * q, z, q >= 0, None, False)
    edges_arrived(rows_of(dd), 4, SEM["dif"], DEEP)
    edges_arrived(rows_of(rr), 4, SEM["gro"], DEEP)
    for r, at in ((OWN, OWN), (BUF - 4, DEEP - 4)):
        aa[r:r + 4] = DIFFUSION * dd[at:at + 4]
        bb[r:r + 4] = STEP * rr[at:at + 4]
    edges_arrived(lead(o10, 3), 3, SEM["o1_0"])
    edges_arrived(lead(ge0, 4), 2, SEM["ge0"])
    edges_arrived(lead(go0, 4), 1, SEM["go0"])

    relax(0, 2, field(o10, 1), 2)
    for c in range(CUTS):
        g = ge0[3, own, cut(c)] + ps[2, :, cut(c)]
        go1[1, own, cut(c)] = g
        o11[1, own, cut(c)] = ee[2, own, cut(c)] + 2.0 * ne[2, own, cut(c)] + g
    send_next(rows_of(o11, 1), rows_of(po, 1), 3, "po1")
    relax(0, 3, field(o10, 2), 3)
    send_next(rows_of(ps, 3), rows_of(pr, 0), 2, "pr0")
    relax(0, 1, field(o10, 0), 1)
    for c in range(CUTS):
        ge1[1, own, cut(c)] = ge0[2, own, cut(c)] + ps[1, :, cut(c)]
    exchange(rows_of(ge1, 1), 2, "ge1")

    all_arrived(rows_of(pv), 4, SEM["pv"])
    all_arrived(rows_of(pg), 3, SEM["pg"])
    for c in range(CUTS):
        n, u = spread(field(pv), c, BUF)
        po[0, :, cut(c)] = u + n + pg[:, cut(c)]
    relax(0, 0, field(po, 0), 0)
    for c in range(CUTS):
        g = ge0[1, own, cut(c)] + ps[0, :, cut(c)]
        go1[0, own, cut(c)] = g
        o11[0, own, cut(c)] = ee[0, own, cut(c)] + 2.0 * ne[0, own, cut(c)] + g
    exchange(rows_of(o11, 0), 3, "o1_1")
    exchange(lead(go1, 2), 1, "go1")

    for k in range(GROUP):
        arrived(ga.at[k, 0:OWN, :], SEM["ga"] + 3 * k)
    slots = lambda r, h: ga.at[:, pl.ds(r, h), :]
    send_edges(slots, slots, 8, SEM["gae"], SEM["gae"], t, None, DEEP)
    edges_arrived(rows_of(ge1, 1), 2, SEM["ge1"])
    edges_arrived(rows_of(o11, 0), 3, SEM["o1_1"])
    edges_arrived(lead(go1, 2), 1, SEM["go1"])
    relax(1, 1, field(o11, 0), 5)
    send_next(rows_of(ps, 5), rows_of(pr, 1), 2, "pr1")
    all_arrived(rows_of(pr, 0), 2, SEM["pr0"])
    ge1[0] = ge0[0] + pr[0]
    all_arrived(rows_of(po, 1), 3, SEM["po1"])
    relax(1, 0, field(po, 1), 4)
    for c in range(CUTS):
        g = ge1[1, own, cut(c)] + ps[4, :, cut(c)]
        go2[0, own, cut(c)] = g
        o12[0, own, cut(c)] = ee[0, own, cut(c)] + 4.0 * ne[0, own, cut(c)] + g
    send_next(rows_of(o12, 0), rows_of(po, 2), 3, "po2")
    exchange(rows_of(go2, 0), 2, "go2")

    for ref, name in ((dd, "dif2"), (rr, "gro2")):
        send(ref.at[8:12, :], ref.at[24:28, :], SEM[name] + 1, SEM[name] + 1, t, s + 1, has_down)
        send(ref.at[4:8, :], ref.at[20:24, :], SEM[name] + 2, SEM[name] + 2, t, s - 1, has_up)
    all_arrived(rows_of(pr, 1), 2, SEM["pr1"])
    ge2[0] = ge1[0] + pr[1]
    edges_arrived(rows_of(go2, 0), 2, SEM["go2"])
    all_arrived(rows_of(po, 2), 3, SEM["po2"])
    relax(2, 0, field(po, 2), 6)

    is_last = t == n_t - 1

    def onward(c0, w):
        at = slice(c0, c0 + w)
        pairs = ps[3, :, at] + ps[5, :, at] + ps[6, :, at]
        return pairs + jnp.where(is_last, ee[0, own, at] + 8.0 * ne[0, own, at], 0.0)

    earlier = list(sent)
    sent.clear()
    stage(onward, xb)
    for k in range(GROUP):
        tm = lax.rem(following + k, n_t)
        send_edges(rows_of(xb, k), rows_of(vin), 8, SEM["old"] + 3 * k, SEM["vin"], tm, is_last, DEEP)
        send(xb.at[k], vin.at[0:OWN, :], SEM["old"] + 3 * k, SEM["vin"], tm, s, is_last)
    k_next = lax.rem(following, GROUP)
    z_next = following // GROUP
    send_group(lambda k: rows_of(xb, k), rows_of(gb, k_next), SEM["gb"], SEM["gb"] + 3 * k_next, z_next,
               q < GROUP - 1, jnp.logical_not(is_last))

    later = list(sent)
    sent[:] = earlier
    settle()
    sent[:] = later

    for ref, name in ((dd, "dif2"), (rr, "gro2")):
        arrived(ref.at[24:28, :], SEM[name] + 1, has_up)
        arrived(ref.at[20:24, :], SEM[name] + 2, has_down)
    lane_deep = lax.broadcasted_iota(jnp.int32, (DEEP, LANES), 1)

    def own_part(k):
        for whole, part, scale in ((dd, ap, DIFFUSION), (rr, bp, STEP)):
            zero = jnp.zeros((DEEP, LANES), F32)
            right = whole[:, (k + 1) * width:(k + 1) * width + LANES] if k < GROUP - 1 else zero
            left = whole[:, k * width - LANES:k * width] if k > 0 else zero
            part[:, 0:width] = scale * whole[:, k * width:(k + 1) * width]
            part[:, width:wide] = scale * jnp.where(lane_deep < LANES // 2, right, left)

    for k in range(GROUP):
        pl.when(mine == k)(functools.partial(own_part, k))

    f = 2.0 ** (len(PAIRS))
    edges_arrived(slots, 8, SEM["gae"], DEEP)
    all_arrived(rows_of(vin), 8, SEM["vin"], DEEP)
    for k in range(GROUP):
        if k == 0:
            arrived(gb.at[0, 0:OWN, :], SEM["gb"], z == 1)
            arrived(gb.at[0, DEEP - 8:DEEP, :], SEM["gb"] + 1, jnp.logical_and(z == 1, has_up))
            arrived(gb.at[0, OWN:OWN + 8, :], SEM["gb"] + 2, jnp.logical_and(z == 1, has_down))
        else:
            all_arrived(rows_of(gb, k), 8, SEM["gb"] + 3 * k, DEEP)
        u = vin[...] if k == 0 else vo[k - 1]
        beside = pltpu.roll(u, 1, 0) + pltpu.roll(u, DEEP - 1, 0) + pltpu.roll(u, 1, 1) + pltpu.roll(u, wide - 1, 1)
        n = ap[...] * (beside - 4.0 * u) + bp[...] * u / (1.0 + u * u)
        u = u + f * n + gb[k]
        if k == 0:
            u = jnp.where(z == 0, vin[...], u)
        vo[k] = u + ga[k]
        if k == GROUP - 1:
            tm = holder(1, mine)
            send_edges(rows_of(vo, k), rows_of(vin), 8, SEM["vin"], SEM["vin"], tm, z == 0, DEEP)
            send(vo.at[k, 0:OWN, :], vin.at[0:OWN, :], SEM["vin"], SEM["vin"], tm, s, z == 0)

        def block(r, h, k=k):
            return vo.at[k, pl.ds(r, h), 0:width]

        place = rows_of(vr, mine)
        tm = z * GROUP + k
        me = q == k

        def keep():
            pltpu.make_async_copy(block(0, OWN), place(0, OWN), rs.at[SEM["vr"] + 3 * mine]).start()
        pl.when(me)(keep)
        send_edges(block, place, 4, SEM["vr"] + 3 * k, SEM["vr"] + 3 * mine, tm)
        send(block(0, OWN), place(0, OWN), SEM["vr"] + 3 * k, SEM["vr"] + 3 * mine, tm, s, jnp.logical_not(me))

    settle()

    for k in range(GROUP):
        all_arrived(rows_of(vr, k), 4, SEM["vr"] + 3 * k)

    def returned(c0, w):
        if w <= width:
            return vr[c0 // width, :, c0 % width:c0 % width + w]
        return jnp.concatenate([vr[c0 // width + i] for i in range(w // width)], axis=1)

    for c in range(CUTS):
        n, u = spread(returned, c, BUF)
        res[0, :, cut(c)] = u[:OWN]
        res[1, :, cut(c)] = (u + n + go0[0, :, cut(c)])[:OWN]
        ee[1, :, cut(c)] = u + 2.0 * n + go1[0, :, cut(c)]
        ee[2, :, cut(c)] = u + 4.0 * n + go2[0, :, cut(c)]
    stores = []

    def store(j):
        copy = pltpu.make_async_copy(res.at[j], out.at[j], ls.at[j])
        copy.start()
        stores.append(copy)

    store(0)
    store(1)
    for c in range(CUTS):
        n, u = spread(field(ee, 2), c, BUF)
        res[4, :, cut(c)] = u[:OWN]
        res[5, :, cut(c)] = (u + n + go0[2, :, cut(c)])[:OWN]
        ee[3, :, cut(c)] = u + 2.0 * n + go1[1, :, cut(c)]
    store(4)
    store(5)
    for j in (1, 3):
        for c in range(CUTS):
            n, u = spread(field(ee, j), c, OWN)
            res[2 * j, :, cut(c)] = u
            res[2 * j + 1, :, cut(c)] = u + n + go0[j, own, cut(c)]
        store(2 * j)
        store(2 * j + 1)
    for copy in stores:
        copy.wait()


def solution(mesh):
    n_t, n_s = mesh.shape["tm"], mesh.shape["space"]

    def body(initial, source, diffusivity, growth):
        cols = initial.shape[2]
        wide = cols // GROUP + LANES

        def full(*n):
            return pltpu.VMEM((*n, BUF, cols), F32)

        def part(*n):
            return pltpu.VMEM((*n, DEEP, wide), F32)

        scratch = [
            full(4), full(4), full(2), full(1), full(4), full(2), full(1), full(4), full(2), full(1),
            full(3), full(2), full(), full(), full(4), full(4), full(), pltpu.VMEM((7, OWN, cols), F32),
            pltpu.VMEM((DEEP, cols), F32), pltpu.VMEM((DEEP, cols), F32), full(), full(),
            pltpu.VMEM((GROUP, OWN, wide), F32), pltpu.VMEM((GROUP, OWN, wide), F32),
            part(GROUP), part(GROUP), part(), part(GROUP), part(), part(),
            pltpu.VMEM((GROUP, BUF, cols // GROUP), F32),
            pltpu.VMEM(initial.shape, F32),
            pltpu.SemaphoreType.DMA((N_SEM,)), pltpu.SemaphoreType.DMA((N_SEM,)), pltpu.SemaphoreType.DMA((14,)),
        ]
        return pl.pallas_call(
            functools.partial(kernel, n_t, n_s, cols),
            out_shape=jax.ShapeDtypeStruct(initial.shape, F32),
            in_specs=[pl.BlockSpec(memory_space=pl.ANY)] * 4,
            out_specs=pl.BlockSpec(memory_space=pl.ANY),
            scratch_shapes=scratch,
            compiler_params=pltpu.CompilerParams(collective_id=0, has_side_effects=True),
        )(initial, source, diffusivity, growth)

    placed = (P("tm", "space", None), P("tm", "space", None), P("space", None), P("space", None))
    return jax.shard_map(body, mesh=mesh, in_specs=placed, out_specs=P("tm", "space", None), check_vma=False)
```

```python
import functools

import jax
import jax.numpy as jnp
from jax import lax
from jax.experimental import pallas as pl
from jax.experimental.pallas import tpu as pltpu
from jax.sharding import PartitionSpec as P

MESH = pl.DeviceIdType.MESH
F32 = jnp.float32
DIFFUSION = 0.03
STEP = 0.02

OWN = 16
BUF = 24
DEEP = 32
LANES = 128
CUTS = 4
GROUP = 8
PAIRS = (4, 2, 1)

_names = [
    ("v0", 3), ("dif", 3), ("gro", 3), ("ge0", 3), ("go0", 3), ("dif2", 3), ("gro2", 3), ("pv", 3), ("pg", 3),
    ("o1_0", 3), ("o1_1", 3), ("ge1", 3), ("go1", 3), ("go2", 3),
    ("po1", 3), ("po2", 3), ("pr0", 3), ("pr1", 3),
    ("ga", 24), ("gae", 3), ("gb", 24), ("vin", 3), ("vr", 24), ("old", 24),
]
SEM = {}
_at = 0
for _name, _count in _names:
    SEM[_name] = _at
    _at += _count
N_SEM = _at


def kernel(n_t, n_s, cols, ini, src, dif, gro, out, v0, ge0, ge1, ge2, go0, go1, go2, o10, o11, o12,
           po, pr, pv, pg, ee, ne, ob, ps, dd, rr, aa, bb, xa, xb, ga, gb, vin, vo, ap, bp, vr, res,
           ss, rs, ls):
    ge, go, o1 = (ge0, ge1, ge2), (go0, go1, go2), (o10, o11, o12)
    span = cols // CUTS
    width = cols // GROUP
    wide = width + LANES
    t, s = lax.axis_index("tm"), lax.axis_index("space")
    z, q = t // GROUP, lax.rem(t, GROUP)

    def holder(group, block):
        return group * GROUP + lax.rem(block + group * (GROUP // 2), GROUP)

    mine = lax.rem(q + z * (GROUP // 2), GROUP)
    following = lax.rem(t + 1, n_t)
    has_up, has_down = s > 0, s < n_s - 1
    sent = []

    def when(cond, fn):
        if cond is None:
            fn()
        else:
            pl.when(cond)(fn)

    def both(a, b):
        return b if a is None else (a if b is None else jnp.logical_and(a, b))

    def send(source, target, si, ri, tm, space, cond=None):
        def copy():
            return pltpu.make_async_remote_copy(
                src_ref=source, dst_ref=target, send_sem=ss.at[si], recv_sem=rs.at[ri],
                device_id={"tm": tm, "space": space}, device_id_type=MESH)
        when(cond, lambda: copy().start())
        sent.append((cond, copy))

    def settle():
        for cond, copy in sent:
            when(cond, lambda copy=copy: copy().wait_send())
        sent.clear()

    def send_edges(source, target, h, si, ri, tm, cond=None, total=BUF):
        send(source(OWN - h, h), target(total - h, h), si + 1, ri + 1, tm, s + 1, both(cond, has_down))
        send(source(0, h), target(OWN, h), si + 2, ri + 2, tm, s - 1, both(cond, has_up))

    def arrived(target, ri, cond=None):
        def wait():
            pltpu.make_async_remote_copy(
                src_ref=target, dst_ref=target, send_sem=ss.at[0], recv_sem=rs.at[ri],
                device_id={"tm": following, "space": s}, device_id_type=MESH).wait_recv()
        when(cond, wait)

    def edges_arrived(target, h, ri, total=BUF):
        arrived(target(total - h, h), ri + 1, has_up)
        arrived(target(OWN, h), ri + 2, has_down)

    def all_arrived(target, h, ri, total=BUF):
        arrived(target(0, OWN), ri)
        edges_arrived(target, h, ri, total)

    def rows_of(ref, *lead):
        return lambda r, h: ref.at[(*lead, pl.ds(r, h), slice(None))]

    loads = []

    def load(source, target):
        copy = pltpu.make_async_copy(source, target, ls.at[len(loads)])
        copy.start()
        loads.append(copy)

    def clear():
        for ref in (v0, ge0, ge1, ge2, go0, go1, go2, o10, o11, o12, po, pr, ga, gb, vr):
            for j in range(ref.shape[0]):
                ref[j, OWN:, :] = jnp.zeros((ref.shape[1] - OWN, ref.shape[2]), F32)
        for ref in (dd, rr, pv, pg, vin):
            ref[OWN:, :] = jnp.zeros((ref.shape[0] - OWN, ref.shape[1]), F32)

    pl.when(jnp.logical_or(s == 0, s == n_s - 1))(clear)

    barrier = pltpu.get_barrier_semaphore()
    last = q // (GROUP - 1)
    peers = (GROUP + GROUP * last + (1 - z) * (1 - last)) * (
        1 + has_up.astype(jnp.int32) + has_down.astype(jnp.int32)) - 1

    def greet(tm, cond_here=None, cond=None):
        for ds, there in ((0, cond_here), (1, has_down), (-1, has_up)):
            when(both(cond, there), lambda ds=ds: pl.semaphore_signal(
                barrier, inc=1, device_id={"tm": tm, "space": s + ds}, device_id_type=MESH))

    greet(lax.rem(z * GROUP + n_t - 1, n_t))
    greet(mine, None, jnp.logical_and(z == 1, mine < GROUP - 1))
    for k in range(GROUP):
        greet(z * GROUP + k, q != k)

    for j in range(4):
        load(ini.at[2 * j], v0.at[j, 0:OWN, :])
    load(dif, dd.at[0:OWN, :])
    load(gro, rr.at[0:OWN, :])
    for j in range(4):
        load(src.at[2 * j], ge0.at[j, 0:OWN, :])
        load(src.at[2 * j + 1], go0.at[j, 0:OWN, :])

    for copy in loads[:6]:
        copy.wait()
    pl.semaphore_wait(barrier, peers)

    def lead(ref, n):
        return lambda r, h: ref.at[0:n, pl.ds(r, h), :]

    def exchange(ref, h, name):
        send_edges(ref, ref, h, SEM[name], SEM[name], t)

    def send_next(source, target, h, name):
        send_edges(source, target, h, SEM[name], SEM[name], following)
        send(source(0, OWN), target(0, OWN), SEM[name], SEM[name], following, s)

    exchange(lead(v0, 3), 1, "v0")
    send_next(rows_of(v0, 3), rows_of(pv), 4, "pv")
    for copy in loads[6:]:
        copy.wait()
    send_next(rows_of(go0, 3), rows_of(pg), 3, "pg")
    send_edges(rows_of(dd), rows_of(dd), 4, SEM["dif"], SEM["dif"], t, None, DEEP)
    send_edges(rows_of(rr), rows_of(rr), 4, SEM["gro"], SEM["gro"], t, None, DEEP)

    lane = lax.broadcasted_iota(jnp.int32, (BUF, LANES), 1)

    def spread(get, c, rows):
        c0 = c * span
        u = get(c0, span)
        west, east = pltpu.roll(u, 1, 1), pltpu.roll(u, span - 1, 1)
        before = pltpu.roll(get(c0 - LANES, LANES), 1, 1) if c > 0 else jnp.zeros((BUF, LANES), F32)
        after = pltpu.roll(get(c0 + span, LANES), LANES - 1, 1) if c < CUTS - 1 else jnp.zeros((BUF, LANES), F32)
        first = jnp.where(lane == 0, before, west[:, :LANES])
        last = jnp.where(lane == LANES - 1, after, east[:, span - LANES:])
        if span > LANES:
            west = jnp.concatenate([first, west[:, LANES:]], axis=1)
            east = jnp.concatenate([east[:, :span - LANES], last], axis=1)
        else:
            west, east = first, last
        north, south = pltpu.roll(u, 1, 0), pltpu.roll(u, BUF - 1, 0)
        u = u[:rows]
        beside = north[:rows] + south[:rows] + west[:rows] + east[:rows]
        n = aa[0:rows, c0:c0 + span] * (beside - 4.0 * u) + bb[0:rows, c0:c0 + span] * u / (1.0 + u * u)
        return n, u

    def cut(c):
        return slice(c * span, (c + 1) * span)

    def field(ref, *lead):
        return lambda c0, w: ref[(*lead, slice(None), slice(c0, c0 + w))]

    def relax(level, j, source, odd_at):
        f = 2.0 ** level
        for c in range(CUTS):
            n, u = spread(source, c, BUF)
            ee[j, :, cut(c)] = u + f * n + ge[level][j, :, cut(c)]
        for c in range(CUTS):
            n, u = spread(field(ee, j), c, BUF)
            ne[j, :, cut(c)] = n
            ob[:, cut(c)] = u + f * n + go[level][j, :, cut(c)]
        for c in range(CUTS):
            n, u = spread(field(ob), c, OWN)
            pair = u + f * n - ee[j, 0:OWN, cut(c)] - 2.0 * f * ne[j, 0:OWN, cut(c)]
            ps[odd_at, :, cut(c)] = pair

    own = slice(0, OWN)

    edges_arrived(lead(v0, 3), 1, SEM["v0"])
    aa[own] = DIFFUSION * dd[own]
    bb[own] = STEP * rr[own]

    def first_odd(j):
        for c in range(CUTS):
            n, u = spread(field(v0, j), c, OWN)
            o10[j, own, cut(c)] = u + n + go0[j, own, cut(c)]

    lax.fori_loop(0, 3, lambda j, x: (first_odd(j), x)[1], 0)
    exchange(lead(o10, 3), 3, "o1_0")
    exchange(lead(ge0, 4), 2, "ge0")
    exchange(lead(go0, 4), 1, "go0")

    def stage(get, target):
        for k in range(GROUP):
            main = get(k * width, width)
            right = get((k + 1) * width, LANES) if k < GROUP - 1 else jnp.zeros((OWN, LANES), F32)
            left = get(k * width - LANES, LANES) if k > 0 else jnp.zeros((OWN, LANES), F32)
            target[k, :, 0:width] = main
            target[k, :, width:wide] = jnp.where(lane[:OWN] < LANES // 2, right, left)

    def send_group(source, target, si, ri, group, itself, cond=None, edges=None):
        for k in range(GROUP):
            tm = holder(group, k)
            me = jnp.logical_and(itself, mine == k)

            def keep(k=k):
                pltpu.make_async_copy(source(k)(0, OWN), target(0, OWN), rs.at[ri]).start()
            pl.when(me)(keep)
            if edges is not None:
                for h, chosen in edges:
                    send_edges(source(k), target, h, si + 3 * k, ri, tm, both(cond, chosen), DEEP)
            send(source(k)(0, OWN), target(0, OWN), si + 3 * k, ri, tm, s, both(cond, jnp.logical_not(me)))

    stage(lambda c0, w: ge0[0, own, c0:c0 + w], xa)
    send_group(lambda k: rows_of(xa, k), rows_of(ga, q), SEM["ga"], SEM["ga"] + 3 * q, z, q >= 0)
    edges_arrived(rows_of(dd), 4, SEM["dif"], DEEP)
    edges_arrived(rows_of(rr), 4, SEM["gro"], DEEP)
    for r, at in ((OWN, OWN), (BUF - 4, DEEP - 4)):
        aa[r:r + 4] = DIFFUSION * dd[at:at + 4]
        bb[r:r + 4] = STEP * rr[at:at + 4]
    edges_arrived(lead(o10, 3), 3, SEM["o1_0"])
    edges_arrived(lead(ge0, 4), 2, SEM["ge0"])
    edges_arrived(lead(go0, 4), 1, SEM["go0"])

    relax(0, 2, field(o10, 1), 2)
    for c in range(CUTS):
        g = ge0[3, own, cut(c)] + ps[2, :, cut(c)]
        go1[1, own, cut(c)] = g
        o11[1, own, cut(c)] = ee[2, own, cut(c)] + 2.0 * ne[2, own, cut(c)] + g
    send_next(rows_of(o11, 1), rows_of(po, 1), 3, "po1")
    relax(0, 3, field(o10, 2), 3)
    send_next(rows_of(ps, 3), rows_of(pr, 0), 2, "pr0")
    relax(0, 1, field(o10, 0), 1)
    for c in range(CUTS):
        ge1[1, own, cut(c)] = ge0[2, own, cut(c)] + ps[1, :, cut(c)]
    exchange(rows_of(ge1, 1), 2, "ge1")

    all_arrived(rows_of(pv), 4, SEM["pv"])
    all_arrived(rows_of(pg), 3, SEM["pg"])
    for c in range(CUTS):
        n, u = spread(field(pv), c, BUF)
        po[0, :, cut(c)] = u + n + pg[:, cut(c)]
    relax(0, 0, field(po, 0), 0)
    for c in range(CUTS):
        g = ge0[1, own, cut(c)] + ps[0, :, cut(c)]
        go1[0, own, cut(c)] = g
        o11[0, own, cut(c)] = ee[0, own, cut(c)] + 2.0 * ne[0, own, cut(c)] + g
    exchange(rows_of(o11, 0), 3, "o1_1")
    exchange(lead(go1, 2), 1, "go1")

    for k in range(GROUP):
        arrived(ga.at[k, 0:OWN, :], SEM["ga"] + 3 * k)
    slots = lambda r, h: ga.at[:, pl.ds(r, h), :]
    send_edges(slots, slots, 8, SEM["gae"], SEM["gae"], t, None, DEEP)
    edges_arrived(rows_of(ge1, 1), 2, SEM["ge1"])
    edges_arrived(rows_of(o11, 0), 3, SEM["o1_1"])
    edges_arrived(lead(go1, 2), 1, SEM["go1"])
    relax(1, 1, field(o11, 0), 5)
    send_next(rows_of(ps, 5), rows_of(pr, 1), 2, "pr1")
    all_arrived(rows_of(pr, 0), 2, SEM["pr0"])
    ge1[0] = ge0[0] + pr[0]
    all_arrived(rows_of(po, 1), 3, SEM["po1"])
    relax(1, 0, field(po, 1), 4)
    for c in range(CUTS):
        g = ge1[1, own, cut(c)] + ps[4, :, cut(c)]
        go2[0, own, cut(c)] = g
        o12[0, own, cut(c)] = ee[0, own, cut(c)] + 4.0 * ne[0, own, cut(c)] + g
    send_next(rows_of(o12, 0), rows_of(po, 2), 3, "po2")
    exchange(rows_of(go2, 0), 2, "go2")

    for ref, name in ((dd, "dif2"), (rr, "gro2")):
        send(ref.at[8:12, :], ref.at[24:28, :], SEM[name] + 1, SEM[name] + 1, t, s + 1, has_down)
        send(ref.at[4:8, :], ref.at[20:24, :], SEM[name] + 2, SEM[name] + 2, t, s - 1, has_up)
    all_arrived(rows_of(pr, 1), 2, SEM["pr1"])
    ge2[0] = ge1[0] + pr[1]
    edges_arrived(rows_of(go2, 0), 2, SEM["go2"])
    all_arrived(rows_of(po, 2), 3, SEM["po2"])
    relax(2, 0, field(po, 2), 6)

    is_last = t == n_t - 1

    def onward(c0, w):
        at = slice(c0, c0 + w)
        pairs = ps[3, :, at] + ps[5, :, at] + ps[6, :, at]
        return pairs + jnp.where(is_last, ee[0, own, at] + 8.0 * ne[0, own, at], 0.0)

    earlier = list(sent)
    sent.clear()
    stage(onward, xb)
    for k in range(GROUP):
        tm = lax.rem(following + k, n_t)
        send_edges(rows_of(xb, k), rows_of(vin), 8, SEM["old"] + 3 * k, SEM["vin"], tm, is_last, DEEP)
        send(xb.at[k], vin.at[0:OWN, :], SEM["old"] + 3 * k, SEM["vin"], tm, s, is_last)
    k_next = lax.rem(following, GROUP)
    z_next = following // GROUP
    send_group(lambda k: rows_of(xb, k), rows_of(gb, k_next), SEM["gb"], SEM["gb"] + 3 * k_next, z_next,
               q < GROUP - 1, jnp.logical_not(is_last), ((7, k_next < 4), (3, k_next >= 4)))

    later = list(sent)
    sent[:] = earlier
    settle()
    sent[:] = later

    for ref, name in ((dd, "dif2"), (rr, "gro2")):
        arrived(ref.at[24:28, :], SEM[name] + 1, has_up)
        arrived(ref.at[20:24, :], SEM[name] + 2, has_down)
    lane_deep = lax.broadcasted_iota(jnp.int32, (DEEP, LANES), 1)

    def own_part(k):
        for whole, part, scale in ((dd, ap, DIFFUSION), (rr, bp, STEP)):
            zero = jnp.zeros((DEEP, LANES), F32)
            right = whole[:, (k + 1) * width:(k + 1) * width + LANES] if k < GROUP - 1 else zero
            left = whole[:, k * width - LANES:k * width] if k > 0 else zero
            part[:, 0:width] = scale * whole[:, k * width:(k + 1) * width]
            part[:, width:wide] = scale * jnp.where(lane_deep < LANES // 2, right, left)

    for k in range(GROUP):
        pl.when(mine == k)(functools.partial(own_part, k))

    f = 2.0 ** (len(PAIRS))
    edges_arrived(slots, 8, SEM["gae"], DEEP)
    all_arrived(rows_of(vin), 8, SEM["vin"], DEEP)
    for k in range(GROUP):
        if k == 0:
            arrived(gb.at[0, 0:OWN, :], SEM["gb"], z == 1)
            arrived(gb.at[0, DEEP - 7:DEEP, :], SEM["gb"] + 1, jnp.logical_and(z == 1, has_up))
            arrived(gb.at[0, OWN:OWN + 7, :], SEM["gb"] + 2, jnp.logical_and(z == 1, has_down))
        else:
            all_arrived(rows_of(gb, k), 7 if k < 4 else 3, SEM["gb"] + 3 * k, DEEP)
        u = vin[...] if k == 0 else vo[k - 1]
        beside = pltpu.roll(u, 1, 0) + pltpu.roll(u, DEEP - 1, 0) + pltpu.roll(u, 1, 1) + pltpu.roll(u, wide - 1, 1)
        n = ap[...] * (beside - 4.0 * u) + bp[...] * u / (1.0 + u * u)
        u = u + f * n + gb[k]
        if k == 0:
            u = jnp.where(z == 0, vin[...], u)
        vo[k] = u + ga[k]
        if k == GROUP - 1:
            tm = holder(1, mine)
            send_edges(rows_of(vo, k), rows_of(vin), 8, SEM["vin"], SEM["vin"], tm, z == 0, DEEP)
            send(vo.at[k, 0:OWN, :], vin.at[0:OWN, :], SEM["vin"], SEM["vin"], tm, s, z == 0)

        def block(r, h, k=k):
            return vo.at[k, pl.ds(r, h), 0:width]

        place = rows_of(vr, mine)
        tm = z * GROUP + k
        me = q == k

        def keep():
            pltpu.make_async_copy(block(0, OWN), place(0, OWN), rs.at[SEM["vr"] + 3 * mine]).start()
        pl.when(me)(keep)
        send_edges(block, place, 4, SEM["vr"] + 3 * k, SEM["vr"] + 3 * mine, tm)
        send(block(0, OWN), place(0, OWN), SEM["vr"] + 3 * k, SEM["vr"] + 3 * mine, tm, s, jnp.logical_not(me))

    settle()

    for k in range(GROUP):
        all_arrived(rows_of(vr, k), 4, SEM["vr"] + 3 * k)

    def returned(c0, w):
        if w <= width:
            return vr[c0 // width, :, c0 % width:c0 % width + w]
        return jnp.concatenate([vr[c0 // width + i] for i in range(w // width)], axis=1)

    for c in range(CUTS):
        n, u = spread(returned, c, BUF)
        res[0, :, cut(c)] = u[:OWN]
        res[1, :, cut(c)] = (u + n + go0[0, :, cut(c)])[:OWN]
        ee[1, :, cut(c)] = u + 2.0 * n + go1[0, :, cut(c)]
        ee[2, :, cut(c)] = u + 4.0 * n + go2[0, :, cut(c)]
    stores = []

    def store(j):
        copy = pltpu.make_async_copy(res.at[j], out.at[j], ls.at[j])
        copy.start()
        stores.append(copy)

    store(0)
    store(1)
    for c in range(CUTS):
        n, u = spread(field(ee, 2), c, BUF)
        res[4, :, cut(c)] = u[:OWN]
        res[5, :, cut(c)] = (u + n + go0[2, :, cut(c)])[:OWN]
        ee[3, :, cut(c)] = u + 2.0 * n + go1[1, :, cut(c)]
    store(4)
    store(5)
    for j in (1, 3):
        for c in range(CUTS):
            n, u = spread(field(ee, j), c, OWN)
            res[2 * j, :, cut(c)] = u
            res[2 * j + 1, :, cut(c)] = u + n + go0[j, own, cut(c)]
        store(2 * j)
        store(2 * j + 1)
    for copy in stores:
        copy.wait()


def solution(mesh):
    n_t, n_s = mesh.shape["tm"], mesh.shape["space"]

    def body(initial, source, diffusivity, growth):
        cols = initial.shape[2]
        wide = cols // GROUP + LANES

        def full(*n):
            return pltpu.VMEM((*n, BUF, cols), F32)

        def part(*n):
            return pltpu.VMEM((*n, DEEP, wide), F32)

        scratch = [
            full(4), full(4), full(2), full(1), full(4), full(2), full(1), full(4), full(2), full(1),
            full(3), full(2), full(), full(), full(4), full(4), full(), pltpu.VMEM((7, OWN, cols), F32),
            pltpu.VMEM((DEEP, cols), F32), pltpu.VMEM((DEEP, cols), F32), full(), full(),
            pltpu.VMEM((GROUP, OWN, wide), F32), pltpu.VMEM((GROUP, OWN, wide), F32),
            part(GROUP), part(GROUP), part(), part(GROUP), part(), part(),
            pltpu.VMEM((GROUP, BUF, cols // GROUP), F32),
            pltpu.VMEM(initial.shape, F32),
            pltpu.SemaphoreType.DMA((N_SEM,)), pltpu.SemaphoreType.DMA((N_SEM,)), pltpu.SemaphoreType.DMA((14,)),
        ]
        return pl.pallas_call(
            functools.partial(kernel, n_t, n_s, cols),
            out_shape=jax.ShapeDtypeStruct(initial.shape, F32),
            in_specs=[pl.BlockSpec(memory_space=pl.ANY)] * 4,
            out_specs=pl.BlockSpec(memory_space=pl.ANY),
            scratch_shapes=scratch,
            compiler_params=pltpu.CompilerParams(collective_id=0, has_side_effects=True),
        )(initial, source, diffusivity, growth)

    placed = (P("tm", "space", None), P("tm", "space", None), P("space", None), P("space", None))
    return jax.shard_map(body, mesh=mesh, in_specs=placed, out_specs=P("tm", "space", None), check_vma=False)
```
